32 devices in a mesh: grp: 2 (over y), pts: 4 (over z), col: 2 (over x), sub: 2 (over core).
Axes of the slice: x: 2, y: 2, z: 4, core: 2. Of those that a mesh axis runs over, the one named last changes fastest.
Arguments:
- points: bfloat16 [32768, 256], P(('grp', 'pts', 'sub')), parts along dimension 0, may hold values from -12 to 12
- weights: bfloat16 [32768, 128], P(('grp', 'pts', 'sub')), parts along dimension 0, may hold values from -0.046875 to 0.046875
- tile_rows: int32 [4, 8, 128], P(('grp', 'col'), ('pts', 'sub')), parts along dimension 0, may hold values from 0 to 2047, as said below
- tile_count: int32 [4, 8], P(('grp', 'col')), parts along dimension 0, may hold values from 1 to 128, 512 in all within a row
- sketch_pick: int32 [4, 256], P(('grp', 'col')), parts along dimension 0, may hold values from 0 to 511, as said below
- block_targets: bfloat16 [4, 1024, 128], P(('grp', 'col'), ('pts', 'sub')), parts along dimension 0, may hold values from -4 to 4
- core_inv: float32 [1024, 512], P('grp'), parts along dimension 0, as said below
Outputs:
- block_grad: float32 [4, 1024, 128], P(('grp', 'col'), ('pts', 'sub')), parts along dimension 0
- direction: float32 [4, 1024, 128], P(('grp', 'col'), ('pts', 'sub')), parts along dimension 0
The draws below stay inside these ranges and needn't reach their ends.
There are 2 independent parts, one for each index of `grp`. The reference program is written for one: setup_inputs(seed, part) draws one part's arguments, and reference() takes and returns one part's arrays. A program takes and returns all parts, laid end to end along the dimension named above; each array names one. Nothing has to cross between parts.
Inputs may be any that keep to these rules, and one draw needn't show every extreme that they name: For each owner o, the 256 entries tile_rows[:, o, :] are distinct; only slots below tile_count are used. `tile_count`: each row of 8 counts sums to 512, and its largest count is 128. `sketch_pick`: the entries of one row are distinct. `core_inv`: A full-rank matrix.
All inputs are finite; a program needn't handle non-finite values.
Results may differ from the reference program's by a relative error of at most 0.0003.
Values may be sent and summed in bfloat16 or wider, within the bound.
No kernel may reach another device: no remote copies, remote signals or barrier semaphores. Data moves between devices by JAX's collectives and lax.ppermute only.
A program may use at most 64 MiB of HBM per device.

```python
import math
import jax
import jax.numpy as jnp
import numpy as np
from jax import lax

DW = 256
OUT = 128
RANK = 512
CAP = 128
PTS_DEV = 2048
OWNERS = 8
TILE = 1024
LIVE = 512
BLOCK = 1024
SKETCH_DEV = 256
NPTS = 16384
N_COL = 2


def draw_points(key, part):
    latent_width = 16
    cluster_total = 8
    base_key = jax.random.fold_in(key, 23)
    center_key, mixing_key, member_key, latent_key, noise_key = jax.random.split(base_key, 5)
    centers = 1.5 * jax.random.normal(center_key, (cluster_total, DW), jnp.float32)
    mixing = jax.random.normal(mixing_key, (latent_width, DW), jnp.float32) / jnp.sqrt(jnp.float32(latent_width))
    member = jax.random.randint(member_key, (NPTS,), 0, cluster_total)
    latent = jax.random.normal(latent_key, (NPTS, latent_width), jnp.float32)
    noise = 0.35 * jax.random.normal(noise_key, (NPTS, DW), jnp.float32)
    onehot = (member[:, None] == jnp.arange(cluster_total)[None, :]).astype(jnp.float32)
    values = jnp.dot(onehot, centers, precision=lax.Precision.HIGHEST)
    values = values + jnp.dot(latent, mixing, precision=lax.Precision.HIGHEST) + noise
    return jnp.clip(values, -12.0, 12.0).astype(jnp.bfloat16)


def draw_tile_rows(key, part):
    owner_keys = jax.random.split(jax.random.fold_in(key, 5), OWNERS)

    def one_owner(owner_key):
        return jax.random.permutation(owner_key, PTS_DEV)[:N_COL * CAP].reshape(N_COL, CAP)
    listed = jax.vmap(one_owner)(owner_keys)
    return jnp.transpose(listed, (1, 0, 2)).astype(jnp.int32)


def draw_sketch_pick(key, part):
    col_keys = jax.random.split(jax.random.fold_in(key, 11), N_COL)

    def one_col(col_key):
        return jax.random.permutation(col_key, LIVE)[:SKETCH_DEV]
    return jax.vmap(one_col)(col_keys).astype(jnp.int32)


def draw_core_inv(key, part):
    diag_key, other_key = jax.random.split(jax.random.fold_in(key, 17))
    diagonal = jax.random.uniform(diag_key, (RANK,), jnp.float32, 1.0, 4.0)
    others = jax.random.normal(other_key, (RANK, RANK), jnp.float32) / jnp.sqrt(jnp.float32(RANK))
    factor = 200.0 / (RANK * jnp.sqrt(jnp.float32(BLOCK)))
    return (factor * (jnp.diag(diagonal) + others)).astype(jnp.float32)


def block_scale(own_key, extent, cuts, low, top_value):
    factor_of, own = 1.0, jax.random.fold_in(own_key, 6)
    for axis_at, shards_of in cuts:
        steps = jnp.exp(jax.random.uniform(jax.random.fold_in(own, axis_at), (shards_of,), jnp.float32, low / len(cuts), top_value / len(cuts)))
        factor_of = factor_of * jnp.repeat(steps, extent[axis_at] // shards_of).reshape([-1 if axis == axis_at else 1 for axis in range(len(extent))])
    return factor_of


def length_profile(number_of, total, bound, lean):
    weights = [(1 << 20) // math.isqrt(standing ** lean) + 1 for standing in range(2, number_of + 1)]
    rest, given = total - bound - (number_of - 1), [1] * (number_of - 1)
    while rest > 0:
        movable = [i for i in range(number_of - 1) if given[i] < bound]
        mass, left = sum([weights[i] for i in movable]), rest
        for i in movable:
            extra = min(bound - given[i], max(1, left * weights[i] // mass), rest)
            given[i] = given[i] + extra
            rest = rest - extra
    return np.array([bound] + given)


def ragged(own_key, count, total, bound, slope):
    if count == 2:
        one = jax.random.randint(own_key, (), max(1, total - bound), min(bound, total - 1) + 1)
        return jnp.stack([one, total - one])
    lengths = jnp.asarray(length_profile(count, total, bound, slope), jnp.int32)
    pairs = (count - 1) // 2
    giver, sink = lengths[1:1 + 2 * pairs:2], lengths[2:2 + 2 * pairs:2]
    slack = jnp.minimum(giver - 1, bound - sink)
    moved = jax.random.randint(jax.random.fold_in(own_key, 1), (pairs,), 0, 1 << 20) % (slack + 1)
    lengths = lengths.at[1:1 + 2 * pairs:2].set(giver - moved).at[2:2 + 2 * pairs:2].set(sink + moved)
    return lengths[jax.random.permutation(jax.random.fold_in(own_key, 2), count)]


def scatter_about(rng, shape, spread, reach, shards=(), held_as=jnp.bfloat16):
    drawn = jax.random.normal(rng, shape, jnp.float32) * spread
    if len(shards) > 0:
        drawn = block_scale(rng, shape, shards, -0.22, 0.18) * drawn
    return jnp.clip(drawn, min=-reach, max=reach).astype(held_as)


def setup_inputs(seed: int = 0, part: int = 0) -> dict:
    splits = jax.random.split(jax.random.key(seed), 8)
    part_keys = jax.random.split(jax.random.fold_in(splits[7], part), 8)
    return {
        "points": draw_points(jax.random.fold_in(jax.random.fold_in(splits[7], part), 71), part),
        "weights": scatter_about(part_keys[1], (NPTS, OUT), NPTS ** -0.5, 0.046875, ((0, 8),)),
        "tile_rows": draw_tile_rows(jax.random.fold_in(jax.random.fold_in(splits[7], part), 71), part),
        "tile_count": jax.vmap(lambda own: ragged(own, OWNERS, LIVE, CAP, 2))(jax.random.split(part_keys[3], N_COL)).reshape((N_COL, OWNERS)).astype(jnp.int32),
        "sketch_pick": draw_sketch_pick(jax.random.fold_in(jax.random.fold_in(splits[7], part), 71), part),
        "block_targets": scatter_about(part_keys[5], (N_COL, TILE, OUT), 0.5, 4.0, ((0, 2), (1, 8))),
        "core_inv": draw_core_inv(jax.random.fold_in(jax.random.fold_in(splits[7], part), 71), part),
    }


RIDGE_COEF = 50.0
HIGHEST_PREC = lax.Precision.HIGHEST


def sq_norms(values):
    widened = values.astype(jnp.float32)
    return jnp.sum(widened * widened, axis=1)


def kernel(left_x, right_x):
    inner_prods = jnp.dot(left_x.astype(jnp.float32), right_x.astype(jnp.float32).T, precision=HIGHEST_PREC)
    dist_sq = sq_norms(left_x)[:, None] + sq_norms(right_x)[None, :] - 2.0 * inner_prods
    return jnp.exp(-dist_sq / DW)


def live_slots(counts):
    offsets = jnp.cumsum(counts) - counts
    rank_ids = jnp.arange(LIVE, dtype=jnp.int32)
    owner_of = jnp.sum((offsets[None, :] <= rank_ids[:, None]).astype(jnp.int32), axis=1) - 1
    return (owner_of * CAP + rank_ids - jnp.take(offsets, owner_of)).astype(jnp.int32)


def reference(points, weights, tile_rows, tile_count, sketch_pick, block_targets, core_inv):
    owner_base = (jnp.arange(OWNERS, dtype=jnp.int32) * PTS_DEV)[None, :, None]
    global_rows = (tile_rows + owner_base).reshape(N_COL, TILE).astype(jnp.int32)
    live_slot = jax.vmap(live_slots)(tile_count)
    live_rows = jnp.take_along_axis(global_rows, live_slot, axis=1).reshape(-1)
    live_x = jnp.take(points, live_rows, axis=0)
    all_sq = sq_norms(points)
    wide_points = points.astype(jnp.float32)
    wide_weights = weights.astype(jnp.float32)

    def rows_term(row_block):
        inner_prods = jnp.dot(row_block.astype(jnp.float32), wide_points.T, precision=HIGHEST_PREC)
        dist_sq = sq_norms(row_block)[:, None] + all_sq[None, :] - 2.0 * inner_prods
        kern_vals = jnp.exp(-dist_sq / DW)
        return jnp.dot(kern_vals, wide_weights, precision=HIGHEST_PREC)

    row_step = math.gcd(BLOCK, 512)
    part_live = lax.map(rows_term, live_x.reshape(BLOCK // row_step, row_step, DW)).reshape(N_COL, LIVE, OUT)
    offsets = jnp.cumsum(tile_count, axis=1) - tile_count
    slot_ids = jnp.arange(CAP, dtype=jnp.int32)
    used_mask = slot_ids[None, None, :] < tile_count[:, :, None]
    rank_of = jnp.minimum(offsets[:, :, None] + slot_ids[None, None, :], LIVE - 1).reshape(N_COL, TILE).astype(jnp.int32)
    slab_sum = jnp.take_along_axis(part_live, rank_of[:, :, None], axis=1)
    used_float = used_mask.reshape(N_COL, TILE, 1).astype(jnp.float32)
    alpha_block = jnp.take(weights, global_rows.reshape(-1), axis=0).astype(jnp.float32).reshape(N_COL, TILE, OUT)
    block_grad = used_float * (slab_sum + RIDGE_COEF * alpha_block - block_targets.astype(jnp.float32))
    sketch_slot = jnp.take_along_axis(live_slot, sketch_pick, axis=1)
    sketch_rows = jnp.take_along_axis(global_rows, sketch_slot, axis=1).reshape(-1)
    sketch_x = jnp.take(points, sketch_rows, axis=0)
    block_x = jnp.take(points, global_rows.reshape(-1), axis=0)
    flat_used = used_float.reshape(-1, 1)
    sketch_kern = kernel(block_x, sketch_x) * flat_used
    flat_grad = block_grad.reshape(-1, OUT)
    projected = jnp.dot(sketch_kern.T, flat_grad, precision=HIGHEST_PREC)
    weighted = jnp.dot(core_inv, projected, precision=HIGHEST_PREC)
    direction = flat_used * (flat_grad - jnp.dot(sketch_kern, weighted, precision=HIGHEST_PREC))
    return block_grad, direction.reshape(N_COL, TILE, OUT)
```

```python
import math

import jax
import jax.numpy as jnp
from jax import lax
from jax.experimental import pallas as pl
from jax.experimental.pallas import tpu as pltpu
from jax.sharding import PartitionSpec as P

RIDGE_COEF = 50.0
LOG2E = 1.4426950408889634
HIGHEST_PREC = lax.Precision.HIGHEST


def sq_norms(values):
    widened = values.astype(jnp.float32)
    return jnp.sum(widened * widened, axis=1)


def kernel_block(left_x, right_x):
    scale = LOG2E / left_x.shape[1]
    inner_prods = jnp.einsum("ik,jk->ij", left_x, right_x, preferred_element_type=jnp.float32)
    return jnp.exp2(
        inner_prods * (2.0 * scale)
        - (sq_norms(left_x) * scale)[:, None]
        - (sq_norms(right_x) * scale)[None, :]
    )


def hop(values, axis, size, step):
    return lax.ppermute(values, axis, [(j, j ^ step) for j in range(size)])


def slab_kernel(n_blocks, half_rows, scalars, *refs):
    blocks = refs[:n_blocks]
    slabs, slab_sqs, slab_ws, shifts = refs[n_blocks : n_blocks + 4]
    part_ref, live_ref, rows, sums = refs[n_blocks + 4 :]
    cap, width = blocks[0].shape
    scale = LOG2E / width

    def place(target, values, rel):
        off, count = scalars[rel], scalars[n_blocks + rel]
        skew = lax.rem(off, 8)
        slot = lax.broadcasted_iota(jnp.int32, (cap + 8, 1), 0)
        kept = (slot >= skew) & (slot < skew + count)
        tail = jnp.zeros((8, values.shape[1]), jnp.float32)
        moved = pltpu.roll(jnp.concatenate([values, tail], axis=0), skew, 0)
        here = pl.ds(pl.multiple_of(off - skew, 8), cap + 8)
        target[here, :] = jnp.where(kept, moved, target[here, :])

    for rel in range(n_blocks):
        place(rows, blocks[rel][...].astype(jnp.float32), rel)
    live_ref[...] = rows[: live_ref.shape[0], :].astype(live_ref.dtype)
    start = pl.multiple_of(scalars[2 * n_blocks] * half_rows, half_rows)
    mine = rows[pl.ds(start, half_rows), :]
    mine_sq = jnp.sum(mine * mine, axis=1, keepdims=True) * scale
    mine_x = mine.astype(jnp.bfloat16)
    sums[...] = jnp.zeros_like(sums)
    for rel in range(shifts.shape[0]):
        place(sums, shifts[rel], rel)
    total = sums[pl.ds(start, half_rows), :]
    step = math.gcd(slabs.shape[1], 512)
    for which in range(slabs.shape[0]):
        for at in range(0, slabs.shape[1], step):
            inner = lax.dot_general(
                mine_x,
                slabs[which, at : at + step, :],
                (((1,), (1,)), ((), ())),
                preferred_element_type=jnp.float32,
            )
            kern = jnp.exp2(
                inner * (2.0 * scale) - mine_sq - slab_sqs[which, :, at : at + step]
            )
            high = kern.astype(jnp.bfloat16)
            low = (kern - high.astype(jnp.float32)).astype(jnp.bfloat16)
            slab_w = slab_ws[which, at : at + step, :]
            total = total + jnp.dot(high, slab_w, preferred_element_type=jnp.float32)
            total = total + jnp.dot(low, slab_w, preferred_element_type=jnp.float32)
    part_ref[...] = total


def make_device(mesh):
    n_pts, n_col, n_sub = mesh.shape["pts"], mesh.shape["col"], mesh.shape["sub"]

    def per_device(points, weights, tile_rows, tile_count, sketch_pick, block_targets, core_inv):
        cap = tile_rows.shape[2]
        width, outs = points.shape[1], weights.shape[1]
        scale = LOG2E / width
        counts = tile_count[0]
        owners = counts.shape[0]
        live = owners * cap // 2
        half = live // n_sub
        pts_at, sub_at, col_at = lax.axis_index("pts"), lax.axis_index("sub"), lax.axis_index("col")
        own_at = pts_at * n_sub + sub_at
        offsets = jnp.cumsum(counts) - counts
        rel_owner = own_at ^ jnp.arange(owners, dtype=jnp.int32)
        rel_hot = rel_owner[:, None] == jnp.arange(owners)[None, :]
        rel_off = jnp.sum(jnp.where(rel_hot, offsets[None, :], 0), axis=1)
        rel_cnt = jnp.sum(jnp.where(rel_hot, counts[None, :], 0), axis=1)
        scalars = jnp.concatenate([rel_off, rel_cnt, sub_at[None].astype(jnp.int32)])
        used = (jnp.arange(cap) < rel_cnt[0]).astype(jnp.float32)[:, None]

        row_hot = (tile_rows[0, 0][:, None] == jnp.arange(points.shape[0])[None, :]).astype(points.dtype)
        own_x = jnp.dot(row_hot, points, preferred_element_type=jnp.float32).astype(points.dtype)
        far = [own_x] + [hop(own_x, "pts", n_pts, i) for i in range(1, n_pts)]
        blocks = []
        for block in far:
            blocks += [block] + [hop(block, "sub", n_sub, i) for i in range(1, n_sub)]

        own_alpha = jnp.dot(row_hot, weights, preferred_element_type=jnp.float32)
        shift = RIDGE_COEF * own_alpha - block_targets[0].astype(jnp.float32)
        shifts = jnp.stack([shift] + [hop(shift, "sub", n_sub, i) for i in range(1, n_sub)])
        slabs = jnp.stack([points] + [hop(points, "sub", n_sub, i) for i in range(1, n_sub)])
        slab_ws = jnp.stack([weights] + [hop(weights, "sub", n_sub, i) for i in range(1, n_sub)])
        wide = slabs.astype(jnp.float32)
        slab_sqs = (jnp.sum(wide * wide, axis=2) * scale)[:, None, :]

        vmem = pl.BlockSpec(memory_space=pltpu.VMEM)
        part, live_x = pl.pallas_call(
            lambda *refs: slab_kernel(owners, half, *refs),
            out_shape=(
                jax.ShapeDtypeStruct((half, outs), jnp.float32),
                jax.ShapeDtypeStruct((live, width), points.dtype),
            ),
            in_specs=[pl.BlockSpec(memory_space=pltpu.SMEM)] + [vmem] * (owners + 4),
            out_specs=(vmem, vmem),
            scratch_shapes=[
                pltpu.VMEM((live + cap + 8, width), jnp.float32),
                pltpu.VMEM((live + cap + 8, outs), jnp.float32),
            ],
            name="slab",
        )(scalars, *blocks, slabs, slab_sqs, slab_ws, shifts)

        step = 1
        while step < n_pts:
            part = part + hop(part, "pts", n_pts, step)
            step *= 2

        pick_hot = (sketch_pick[0][:, None] == jnp.arange(live)[None, :]).astype(points.dtype)
        sketch_own = jnp.dot(pick_hot, live_x, preferred_element_type=jnp.float32).astype(points.dtype)
        mine_x = lax.dynamic_slice_in_dim(live_x, sub_at * half, half, 0)
        peer_x = [lax.dynamic_slice_in_dim(live_x, (sub_at ^ i) * half, half, 0) for i in range(n_sub)]
        sent = jnp.concatenate([mine_x, sketch_own], axis=0)
        got = [hop(sent, "col", n_col, i) for i in range(1, n_col)]
        rows_all = list(peer_x)
        for block in got:
            rows_all += [block[:half]] + [hop(block[:half], "sub", n_sub, i) for i in range(1, n_sub)]
        rows_all = jnp.concatenate(rows_all, axis=0)
        sketch_rel = jnp.stack([sketch_own] + [block[half:] for block in got])
        sketch_x = jnp.take(sketch_rel, col_at ^ jnp.arange(n_col), axis=0).reshape(-1, width)

        sketch_kern = used * kernel_block(own_x, sketch_x)
        sketch_all = kernel_block(rows_all, sketch_x)
        mixed = jnp.dot(sketch_kern, core_inv, precision=HIGHEST_PREC)
        gram = jnp.dot(mixed, sketch_all.T, precision=HIGHEST_PREC)

        tile_part = [part] + [hop(part, "sub", n_sub, i) for i in range(1, n_sub)]
        grads = list(tile_part)
        for i in range(1, n_col):
            other = hop(part, "col", n_col, i)
            grads += [other] + [hop(other, "sub", n_sub, j) for j in range(1, n_sub)]
        grads_all = jnp.concatenate(grads, axis=0)
        in_order = jnp.take(jnp.stack(tile_part), sub_at ^ jnp.arange(n_sub), axis=0).reshape(live, outs)
        in_order = jnp.concatenate([in_order, jnp.zeros((cap, outs), jnp.float32)], axis=0)
        block_grad = used * lax.dynamic_slice_in_dim(in_order, rel_off[0], cap, 0)
        direction = used * (block_grad - jnp.dot(gram, grads_all, precision=HIGHEST_PREC))
        return (block_grad[None], direction[None])

    return per_device


def solution(mesh):
    in_specs = (
        P(("grp", "pts", "sub"), None),
        P(("grp", "pts", "sub"), None),
        P(("grp", "col"), ("pts", "sub"), None),
        P(("grp", "col"), None),
        P(("grp", "col"), None),
        P(("grp", "col"), ("pts", "sub"), None),
        P("grp", None),
    )
    out_specs = (P(("grp", "col"), ("pts", "sub"), None), P(("grp", "col"), ("pts", "sub"), None))
    return jax.shard_map(
        make_device(mesh), mesh=mesh, in_specs=in_specs, out_specs=out_specs, check_vma=False
    )
```

```python
import math

import jax
import jax.numpy as jnp
from jax import lax
from jax.experimental import pallas as pl
from jax.experimental.pallas import tpu as pltpu
from jax.sharding import PartitionSpec as P

RIDGE_COEF = 50.0
LOG2E = 1.4426950408889634
VMEM_LIMIT = 24 << 20
ROWS_ROWS = (((1,), (1,)), ((), ()))
VMEM = pl.BlockSpec(memory_space=pltpu.VMEM)
SMEM = pl.BlockSpec(memory_space=pltpu.SMEM)


def split(values):
    high = values.astype(jnp.bfloat16)
    return high, (values - high.astype(jnp.float32)).astype(jnp.bfloat16)


def dot(left, right, dims=(((1,), (0,)), ((), ()))):
    return lax.dot_general(left, right, dims, preferred_element_type=jnp.float32)


def dot_parts(left, right, dims=(((1,), (0,)), ((), ()))):
    return dot(left[0], right[0], dims) + (dot(left[0], right[1], dims) + dot(left[1], right[0], dims))


def row_sq(points, scale):
    wide = points.astype(jnp.float32)
    high, low = split(wide * wide)
    ones = jnp.ones((8, points.shape[1]), jnp.bfloat16)
    return (dot(ones, high, ROWS_ROWS) + dot(ones, low, ROWS_ROWS))[:1] * scale


def col_sq(points, scale):
    wide = points.astype(jnp.float32)
    return jnp.sum(wide * wide, axis=1, keepdims=True) * scale


def as_column(row):
    lanes = 128
    square = [
        jnp.transpose(jnp.broadcast_to(row[:, at : at + lanes], (lanes, lanes)))[:, :1]
        for at in range(0, row.shape[1], lanes)
    ]
    return jnp.concatenate(square, axis=0)


def owner_span(counts, owner):
    off = jnp.int32(0)
    count = jnp.int32(0)
    for at in range(counts.shape[1]):
        here = counts[0, at]
        off = off + jnp.where(at < owner, here, 0)
        count = count + jnp.where(at == owner, here, 0)
    return off, count


def own_kernel(rows_ref, points_ref, own_ref):
    total, width = points_ref.shape
    cap = own_ref.shape[0]
    step = math.gcd(total, 256)
    row_ids = as_column(rows_ref[...])
    own = jnp.zeros((cap, width), jnp.float32)
    for at in range(0, total, step):
        slot = lax.broadcasted_iota(jnp.int32, (cap, step), 1) + at
        hot = (row_ids == slot).astype(jnp.float32).astype(jnp.bfloat16)
        own = own + dot(hot, points_ref[at : at + step, :])
    own_ref[...] = own.astype(own_ref.dtype)


def prep_kernel(rows_ref, points_ref, weights_ref, targets_ref, shift_ref, sq_ref):
    total, width = points_ref.shape
    cap = targets_ref.shape[0]
    step = math.gcd(total, 256)
    row_ids = as_column(rows_ref[...])
    alpha = jnp.zeros((cap, weights_ref.shape[1]), jnp.float32)
    for at in range(0, total, step):
        slot = lax.broadcasted_iota(jnp.int32, (cap, step), 1) + at
        hot = (row_ids == slot).astype(jnp.float32).astype(jnp.bfloat16)
        alpha = alpha + dot(hot, weights_ref[at : at + step, :])
        sq_ref[:, at : at + step] = row_sq(points_ref[at : at + step, :], LOG2E / width)
    shift_ref[...] = RIDGE_COEF * alpha - targets_ref[...].astype(jnp.float32)


def slab_kernel(n_blocks, n_sub, half, counts, *refs):
    blocks, refs = refs[:n_blocks], refs[n_blocks:]
    slabs, slab_sqs = refs[:n_sub], refs[n_sub : 2 * n_sub]
    slab_ws, shifts = refs[2 * n_sub : 3 * n_sub], refs[3 * n_sub : 4 * n_sub]
    part_ref, live_ref, rows, sums = refs[4 * n_sub :]
    cap, width = blocks[0].shape
    scale = LOG2E / width
    sub_at = lax.axis_index("sub")
    own_at = lax.axis_index("pts") * n_sub + sub_at

    def place(target, values, rel):
        off, count = owner_span(counts, own_at ^ rel)
        skew = lax.rem(off, 8)
        slot = lax.broadcasted_iota(jnp.int32, (cap + 8, 1), 0)
        kept = (slot >= skew) & (slot < skew + count)
        tail = jnp.zeros((8, values.shape[1]), jnp.float32)
        moved = pltpu.roll(jnp.concatenate([values, tail], axis=0), skew, 0)
        here = pl.ds(pl.multiple_of(off - skew, 8), cap + 8)
        target[here, :] = jnp.where(kept, moved, target[here, :])

    for rel in range(n_blocks):
        place(rows, blocks[rel][...].astype(jnp.float32), rel)
    live_ref[...] = rows[: live_ref.shape[0], :].astype(live_ref.dtype)
    start = pl.multiple_of(sub_at * half, half)
    mine = rows[pl.ds(start, half), :]
    mine_sq = jnp.sum(mine * mine, axis=1, keepdims=True) * scale
    mine_x = mine.astype(jnp.bfloat16)
    sums[...] = jnp.zeros_like(sums)
    for rel in range(n_sub):
        place(sums, shifts[rel][...], rel)
    total = sums[pl.ds(start, half), :]
    step = math.gcd(slabs[0].shape[0], 512)
    for which in range(n_sub):
        for at in range(0, slabs[which].shape[0], step):
            inner = dot(mine_x, slabs[which][at : at + step, :], ROWS_ROWS)
            kern = jnp.exp2(inner * (2.0 * scale) - mine_sq - slab_sqs[which][:, at : at + step])
            high, low = split(kern)
            slab_w = slab_ws[which][at : at + step, :]
            total = total + dot(high, slab_w)
            total = total + dot(low, slab_w)
    part_ref[...] = total


def pick_kernel(n_sub, half, pick_ref, live_ref, sent_ref, sketch_ref):
    live = live_ref.shape[0]
    share = sketch_ref.shape[0] // n_sub
    sub_at = lax.axis_index("sub")
    slot = lax.broadcasted_iota(jnp.int32, (sketch_ref.shape[0], live), 1)
    hot = (as_column(pick_ref[...]) == slot).astype(jnp.float32).astype(jnp.bfloat16)
    sketch_ref[...] = dot(hot, live_ref[...]).astype(sketch_ref.dtype)
    sent_ref[:half, :] = live_ref[pl.ds(pl.multiple_of(sub_at * half, half), half), :]
    sent_ref[half:, :] = sketch_ref[pl.ds(pl.multiple_of(sub_at * share, share), share), :]


def gram_kernel(n_sub, n_col, half, counts, *refs):
    own_ref, live_ref, sketch_ref, core_ref = refs[:4]
    got, refs = refs[4 : 4 + (n_col - 1) * n_sub], refs[4 + (n_col - 1) * n_sub :]
    outs, sketch_x = refs[:-1], refs[-1]
    cap, width = own_ref.shape
    picks = sketch_ref.shape[0]
    share = picks // n_sub
    scale = LOG2E / width
    sub_at, col_at = lax.axis_index("sub"), lax.axis_index("col")
    own_at = lax.axis_index("pts") * n_sub + sub_at
    count = owner_span(counts, own_at)[1]
    sketch_x[pl.ds(pl.multiple_of(col_at * picks, picks), picks), :] = sketch_ref[...]
    for col in range(1, n_col):
        for sub in range(n_sub):
            to = (col_at ^ col) * picks + (sub_at ^ sub) * share
            block = got[(col - 1) * n_sub + sub][half:, :]
            sketch_x[pl.ds(pl.multiple_of(to, share), share), :] = block
    points = sketch_x[...]
    points_sq = row_sq(points, scale)

    def kern_of(rows):
        inner = dot(rows, points, ROWS_ROWS)
        return jnp.exp2(inner * (2.0 * scale) - col_sq(rows, scale) - points_sq)

    used = lax.broadcasted_iota(jnp.int32, (cap, 1), 0) < count
    own = jnp.where(used, kern_of(own_ref[...]), 0.0)
    mixed = split(dot_parts(split(own), split(core_ref[...])))
    for at in range(n_col * n_sub):
        if at < n_sub:
            rows = live_ref[pl.ds(pl.multiple_of((sub_at ^ at) * half, half), half), :]
        else:
            rows = got[at - n_sub][:half, :]
        high, low = split(dot_parts(mixed, split(kern_of(rows)), ROWS_ROWS))
        outs[2 * at][...] = high
        outs[2 * at + 1][...] = low


def tile_kernel(n_sub, half, counts, *refs):
    parts, grams = refs[:n_sub], refs[n_sub : 3 * n_sub]
    grad_ref, start_ref, ordered = refs[3 * n_sub :]
    cap = grad_ref.shape[0]
    sub_at = lax.axis_index("sub")
    off, count = owner_span(counts, lax.axis_index("pts") * n_sub + sub_at)
    used = lax.broadcasted_iota(jnp.int32, (cap, 1), 0) < count
    for sub in range(n_sub):
        here = pl.ds(pl.multiple_of((sub_at ^ sub) * half, half), half)
        ordered[here, :] = parts[sub][...]
    skew = lax.rem(off, 8)
    rows = ordered[pl.ds(pl.multiple_of(off - skew, 8), cap + 8), :]
    rows = pltpu.roll(rows, lax.rem(cap + 8 - skew, cap + 8), 0)[:cap]
    grad = jnp.where(used, rows, 0.0)
    grad_ref[...] = grad
    for sub in range(n_sub):
        grad = grad - dot_parts((grams[2 * sub][...], grams[2 * sub + 1][...]), split(parts[sub][...]))
    start_ref[...] = jnp.where(used, grad, 0.0)


def rest_kernel(n_sub, counts, start_ref, *refs):
    grams, others, out_ref = refs[: 2 * (len(refs) // 3)], refs[2 * (len(refs) // 3) : -1], refs[-1]
    count = owner_span(counts, lax.axis_index("pts") * n_sub + lax.axis_index("sub"))[1]
    used = lax.broadcasted_iota(jnp.int32, (out_ref.shape[0], 1), 0) < count
    total = start_ref[...]
    for at, other in enumerate(others):
        total = total - dot_parts((grams[2 * at][...], grams[2 * at + 1][...]), split(other[...]))
    out_ref[...] = jnp.where(used, total, 0.0)


def make_device(mesh):
    n_pts, n_col, n_sub = mesh.shape["pts"], mesh.shape["col"], mesh.shape["sub"]

    def hop(values, axis, step):
        return lax.ppermute(values, axis, [(j, j ^ step) for j in range(mesh.shape[axis])])

    def near_of(values):
        return [values] + [hop(values, "sub", i) for i in range(1, n_sub)]

    def call(kernel, out_shape, smem, arrays, scratch=()):
        return pl.pallas_call(
            kernel,
            out_shape=out_shape,
            in_specs=[SMEM] * len(smem) + [VMEM] * len(arrays),
            out_specs=jax.tree.map(lambda _: VMEM, out_shape),
            scratch_shapes=list(scratch),
            compiler_params=pltpu.CompilerParams(vmem_limit_bytes=VMEM_LIMIT),
        )(*smem, *arrays)

    def per_device(points, weights, tile_rows, tile_count, sketch_pick, block_targets, core_inv):
        return body(points, weights, tile_rows, tile_count, sketch_pick, block_targets, core_inv)

    def body(points, weights, tile_rows, tile_count, sketch_pick, block_targets, core_inv):
        cap = tile_rows.shape[2]
        width, outs = points.shape[1], weights.shape[1]
        owners = tile_count.shape[1]
        live = owners * cap // 2
        half = live // n_sub
        picks = sketch_pick.shape[1]

        def f32(*shape):
            return jax.ShapeDtypeStruct(shape, jnp.float32)

        def bf16(*shape):
            return jax.ShapeDtypeStruct(shape, jnp.bfloat16)

        row_ids = tile_rows[0]
        own_x = call(own_kernel, bf16(cap, width), (), (row_ids, points))
        far = [own_x] + [hop(own_x, "pts", i) for i in range(1, n_pts)]
        slabs = near_of(points)
        slab_ws = near_of(weights)
        shift, slab_sq = call(
            prep_kernel, (f32(cap, outs), f32(1, points.shape[0])), (),
            (row_ids, points, weights, block_targets[0]),
        )
        shifts = near_of(shift)
        slab_sqs = near_of(slab_sq)
        blocks = []
        for at, block in enumerate(far):
            blocks += near_of(block)
        part, live_x = call(
            lambda *refs: slab_kernel(owners, n_sub, half, *refs),
            (f32(half, outs), bf16(live, width)),
            (tile_count,),
            (*blocks, *slabs, *slab_sqs, *slab_ws, *shifts),
            (pltpu.VMEM((live + cap + 8, width), jnp.float32), pltpu.VMEM((live + cap + 8, outs), jnp.float32)),
        )

        step = 1
        while step < n_pts:
            part = part + hop(part, "pts", step)
            step *= 2

        sent, sketch = call(
            lambda *refs: pick_kernel(n_sub, half, *refs),
            (bf16(half + picks // n_sub, width), bf16(picks, width)),
            (),
            (sketch_pick, live_x),
        )
        got = []
        for i in range(1, n_col):
            got += near_of(hop(sent, "col", i))
        grams = call(
            lambda *refs: gram_kernel(n_sub, n_col, half, *refs),
            (bf16(cap, half),) * (2 * n_col * n_sub),
            (tile_count,),
            (own_x, live_x, sketch, core_inv, *got),
            (pltpu.VMEM((n_col * picks, width), jnp.bfloat16),),
        )

        parts = near_of(part)
        block_grad, total = call(
            lambda *refs: tile_kernel(n_sub, half, *refs),
            (f32(cap, outs), f32(cap, outs)),
            (tile_count,),
            (*parts, *grams[: 2 * n_sub]),
            (pltpu.VMEM((live + cap + 8, outs), jnp.float32),),
        )
        first, later, first_grams, later_grams = [], [], [], []
        for i in range(1, n_col):
            other = near_of(hop(part, "col", i))
            at = 2 * i * n_sub
            first += other[:1]
            first_grams += grams[at : at + 2]
            later += other[1:]
            later_grams += grams[at + 2 : at + 2 * n_sub]
        rest = lambda *refs: rest_kernel(n_sub, *refs)
        total = call(rest, f32(cap, outs), (tile_count,), (total, *first_grams, *first))
        direction = call(rest, f32(cap, outs), (tile_count,), (total, *later_grams, *later))
        return (block_grad[None], direction[None])

    return per_device


def solution(mesh):
    in_specs = (
        P(("grp", "pts", "sub"), None),
        P(("grp", "pts", "sub"), None),
        P(("grp", "col"), ("pts", "sub"), None),
        P(("grp", "col"), None),
        P(("grp", "col"), None),
        P(("grp", "col"), ("pts", "sub"), None),
        P("grp", None),
    )
    out_specs = (P(("grp", "col"), ("pts", "sub"), None), P(("grp", "col"), ("pts", "sub"), None))
    return jax.shard_map(
        make_device(mesh), mesh=mesh, in_specs=in_specs, out_specs=out_specs, check_vma=False
    )
```

```python
import math

import jax
import jax.numpy as jnp
from jax import lax
from jax.experimental import pallas as pl
from jax.experimental.pallas import tpu as pltpu
from jax.sharding import PartitionSpec as P

RIDGE_COEF = 50.0
LOG2E = 1.4426950408889634
VMEM_LIMIT = 24 << 20
ROWS_ROWS = (((1,), (1,)), ((), ()))
VMEM = pl.BlockSpec(memory_space=pltpu.VMEM)
SMEM = pl.BlockSpec(memory_space=pltpu.SMEM)


def split(values):
    high = values.astype(jnp.bfloat16)
    return high, (values - high.astype(jnp.float32)).astype(jnp.bfloat16)


def dot(left, right, dims=(((1,), (0,)), ((), ()))):
    return lax.dot_general(left, right, dims, preferred_element_type=jnp.float32)


def dot_parts(left, right, dims=(((1,), (0,)), ((), ()))):
    return dot(left[0], right[0], dims) + (dot(left[0], right[1], dims) + dot(left[1], right[0], dims))


def row_sq(points, scale):
    wide = points.astype(jnp.float32)
    high, low = split(wide * wide)
    ones = jnp.ones((8, points.shape[1]), jnp.bfloat16)
    return (dot(ones, high, ROWS_ROWS) + dot(ones, low, ROWS_ROWS))[:1] * scale


def col_sq(points, scale):
    wide = points.astype(jnp.float32)
    return jnp.sum(wide * wide, axis=1, keepdims=True) * scale


def as_column(row):
    lanes = 128
    square = [
        jnp.transpose(jnp.broadcast_to(row[:, at : at + lanes], (lanes, lanes)))[:, :1]
        for at in range(0, row.shape[1], lanes)
    ]
    return jnp.concatenate(square, axis=0)


def owner_span(counts, owner):
    off = jnp.int32(0)
    count = jnp.int32(0)
    for at in range(counts.shape[1]):
        here = counts[0, at]
        off = off + jnp.where(at < owner, here, 0)
        count = count + jnp.where(at == owner, here, 0)
    return off, count


def one_hot(row_ids, at, step):
    slot = lax.broadcasted_iota(jnp.int32, (row_ids.shape[0], step), 1) + at
    return (row_ids == slot).astype(jnp.float32).astype(jnp.bfloat16)


def own_kernel(rows_hbm, points_hbm, own_ref, rows_ref, points_ref, rows_sem, points_sem):
    total, width = points_ref.shape
    cap = own_ref.shape[0]
    step = math.gcd(total, 256)
    rows_copy = pltpu.make_async_copy(rows_hbm, rows_ref, rows_sem)
    points_copy = pltpu.make_async_copy(points_hbm, points_ref, points_sem)
    rows_copy.start()
    points_copy.start()
    rows_copy.wait()
    row_ids = as_column(rows_ref[...])
    points_copy.wait()
    own = jnp.zeros((cap, width), jnp.float32)
    for at in range(0, total, step):
        own = own + dot(one_hot(row_ids, at, step), points_ref[at : at + step, :])
    own_ref[...] = own.astype(own_ref.dtype)


def prep_kernel(rows_ref, weights_ref, targets_ref, shift_ref, turned_ref):
    total = weights_ref.shape[0]
    step = math.gcd(total, 256)
    row_ids = as_column(rows_ref[...])
    alpha = jnp.zeros(shift_ref.shape, jnp.float32)
    for at in range(0, total, step):
        part = weights_ref[at : at + step, :]
        alpha = alpha + dot(one_hot(row_ids, at, step), part)
        turned_ref[:, at : at + step] = jnp.transpose(part.astype(jnp.float32)).astype(jnp.bfloat16)
    shift_ref[...] = RIDGE_COEF * alpha - targets_ref[...].astype(jnp.float32)


def norm_kernel(points_ref, sq_ref):
    sq_ref[...] = col_sq(points_ref[...], LOG2E / points_ref.shape[1])


def slab_kernel(n_blocks, n_sub, quarter, counts, *refs):
    blocks, refs = refs[:n_blocks], refs[n_blocks:]
    slabs, slab_sqs = refs[:n_sub], refs[n_sub : 2 * n_sub]
    slab_ws, shifts = refs[2 * n_sub : 3 * n_sub], refs[3 * n_sub : 4 * n_sub]
    keep_ref, send_ref, live_ref, rows, sums = refs[4 * n_sub :]
    cap, width = blocks[0].shape
    scale = LOG2E / width
    pts_at, sub_at = lax.axis_index("pts"), lax.axis_index("sub")
    own_at = pts_at * n_sub + sub_at

    def place(target, values, rel):
        off, count = owner_span(counts, own_at ^ rel)
        skew = lax.rem(off, 8)
        slot = lax.broadcasted_iota(jnp.int32, (cap + 8, 1), 0)
        kept = (slot >= skew) & (slot < skew + count)
        source = lax.broadcasted_iota(jnp.int32, (cap + 8, cap), 1) + skew
        move = (lax.broadcasted_iota(jnp.int32, (cap + 8, cap), 0) == source)
        move = move.astype(jnp.float32).astype(jnp.bfloat16)
        moved = sum(dot(move, part) for part in values)
        here = pl.ds(pl.multiple_of(off - skew, 8), cap + 8)
        target[here, :] = jnp.where(kept, moved, target[here, :])

    for rel in range(n_blocks):
        place(rows, [blocks[rel][...]], rel)
    live_ref[...] = rows[: live_ref.shape[0], :].astype(live_ref.dtype)
    sums[...] = jnp.zeros_like(sums)
    for rel in range(n_sub):
        high, low = split(shifts[rel][...])
        rest = shifts[rel][...] - high.astype(jnp.float32) - low.astype(jnp.float32)
        place(sums, [high, low, rest.astype(jnp.bfloat16)], rel)
    base = (sub_at * 2 + pts_at % 2) * quarter
    keep = pl.ds(pl.multiple_of(base, quarter), quarter)
    send = pl.ds(pl.multiple_of((sub_at * 2 + 1 - pts_at % 2) * quarter, quarter), quarter)
    mine_x = jnp.concatenate([rows[keep, :], rows[send, :]], axis=0).astype(jnp.bfloat16)
    mine_sq = row_sq(mine_x, scale)
    total = jnp.zeros((keep_ref.shape[1], 2 * quarter), jnp.float32)
    step = math.gcd(slabs[0].shape[0], 256)
    for which in range(n_sub):
        for at in range(0, slabs[which].shape[0], step):
            inner = dot(slabs[which][at : at + step, :], mine_x, ROWS_ROWS)
            kern = jnp.exp2(inner * (2.0 * scale) - mine_sq - slab_sqs[which][at : at + step, :])
            high, low = split(kern)
            turned = slab_ws[which][:, at : at + step]
            total = total + dot(turned, high) + dot(turned, low)
    total = jnp.transpose(total)
    keep_ref[...] = total[:quarter] + sums[keep, :]
    send_ref[...] = total[quarter:] + sums[send, :]


def pick_kernel(half, pick_ref, live_ref, rows_ref, share_ref, sketch_ref):
    live = live_ref.shape[0]
    share = share_ref.shape[0]
    sub_at = lax.axis_index("sub")
    hot = one_hot(as_column(pick_ref[...]), 0, live)
    sketch_ref[...] = dot(hot, live_ref[...]).astype(sketch_ref.dtype)
    rows_ref[...] = live_ref[pl.ds(pl.multiple_of(sub_at * half, half), half), :]
    share_ref[...] = sketch_ref[pl.ds(pl.multiple_of(sub_at * share, share), share), :]


def sketch_rows(rows, points, points_sq):
    inner = dot(rows, points, ROWS_ROWS)
    scale = LOG2E / rows.shape[1]
    return jnp.exp2(inner * (2.0 * scale) - col_sq(rows, scale) - points_sq)


def gram_group(mixed, points, points_sq, blocks, high_ref, low_ref):
    parts = split(sketch_rows(jnp.concatenate(blocks, axis=0), points, points_sq))
    high_ref[...], low_ref[...] = split(dot_parts(mixed, parts, ROWS_ROWS))


def near_gram_kernel(n_sub, n_col, quarter, groups, counts, *refs):
    own_ref, live_ref, sketch_ref, core_ref = refs[:4]
    got, refs = refs[4 : 4 + (n_col - 1) * n_sub], refs[4 + (n_col - 1) * n_sub :]
    sketch_x, mixed_high, mixed_low, outs = refs[0], refs[1], refs[2], refs[3:]
    cap, width = own_ref.shape
    picks = sketch_ref.shape[0]
    share = picks // n_sub
    pts_at, sub_at, col_at = lax.axis_index("pts"), lax.axis_index("sub"), lax.axis_index("col")
    count = owner_span(counts, pts_at * n_sub + sub_at)[1]
    sketch_x[pl.ds(pl.multiple_of(col_at * picks, picks), picks), :] = sketch_ref[...]
    for col in range(1, n_col):
        for sub in range(n_sub):
            to = (col_at ^ col) * picks + (sub_at ^ sub) * share
            sketch_x[pl.ds(pl.multiple_of(to, share), share), :] = got[(col - 1) * n_sub + sub][...]
    points = sketch_x[...]
    points_sq = row_sq(points, LOG2E / width)
    used = lax.broadcasted_iota(jnp.int32, (cap, 1), 0) < count
    own = jnp.where(used, sketch_rows(own_ref[...], points, points_sq), 0.0)
    mixed = split(dot_parts(split(own), split(core_ref[...])))
    mixed_high[...], mixed_low[...] = mixed
    for at, group in enumerate(groups):
        blocks = []
        for _, pts, sub in group:
            base = ((sub_at ^ sub) * 2 + (pts_at % 2 ^ pts)) * quarter
            blocks.append(live_ref[pl.ds(pl.multiple_of(base, quarter), quarter), :])
        gram_group(mixed, points, points_sq, blocks, *outs[2 * at : 2 * at + 2])


def far_gram_kernel(n_sub, quarter, groups, *refs):
    sketch_x, mixed_high, mixed_low = refs[:3]
    got, outs = refs[3 : -2 * len(groups)], refs[-2 * len(groups) :]
    pts_at = lax.axis_index("pts")
    points = sketch_x[...]
    points_sq = row_sq(points, LOG2E / points.shape[1])
    for at, group in enumerate(groups):
        blocks = []
        for col, pts, sub in group:
            base = (pts_at % 2 ^ pts) * quarter
            blocks.append(got[(col - 1) * n_sub + sub][pl.ds(pl.multiple_of(base, quarter), quarter), :])
        mixed = (mixed_high[...], mixed_low[...])
        gram_group(mixed, points, points_sq, blocks, *outs[2 * at : 2 * at + 2])


def apply_grams(grams, parts):
    total, at = None, 0
    for high, low in grams:
        many = high.shape[1] // parts[0].shape[0]
        right = split(jnp.concatenate([ref[...] for ref in parts[at : at + many]], axis=0))
        term = dot_parts((high[...], low[...]), right)
        total = term if total is None else total + term
        at += many
    return total


def part_kernel(n_grams, *refs):
    grams = [refs[2 * at : 2 * at + 2] for at in range(n_grams)]
    refs[-1][...] = apply_grams(grams, refs[2 * n_grams : -1])


def last_kernel(n_sub, n_early, n_grams, counts, *refs):
    early, refs = refs[:n_early], refs[n_early:]
    grams, refs = [refs[2 * at : 2 * at + 2] for at in range(n_grams)], refs[2 * n_grams :]
    tile, later, refs = refs[: 2 * n_sub], refs[2 * n_sub : -3], refs[-3:]
    grad_ref, out_ref, ordered = refs
    cap = grad_ref.shape[0]
    quarter = tile[0].shape[0]
    pts_at, sub_at = lax.axis_index("pts"), lax.axis_index("sub")
    off, count = owner_span(counts, pts_at * n_sub + sub_at)
    used = lax.broadcasted_iota(jnp.int32, (cap, 1), 0) < count
    for at in range(2 * n_sub):
        to = ((sub_at ^ (at % n_sub)) * 2 + (pts_at % 2 ^ (at // n_sub))) * quarter
        ordered[pl.ds(pl.multiple_of(to, quarter), quarter), :] = tile[at][...]
    skew = lax.rem(off, 8)
    rows = ordered[pl.ds(pl.multiple_of(off - skew, 8), cap + 8), :]
    rows = pltpu.roll(rows, lax.rem(cap + 8 - skew, cap + 8), 0)[:cap]
    grad = jnp.where(used, rows, 0.0)
    grad_ref[...] = grad
    for ref in early:
        grad = grad - ref[...]
    out_ref[...] = jnp.where(used, grad - apply_grams(grams, later), 0.0)


def make_device(mesh):
    n_pts, n_col, n_sub = mesh.shape["pts"], mesh.shape["col"], mesh.shape["sub"]

    def hop(values, axis, step):
        axes = axis if isinstance(axis, tuple) else (axis,)
        size = math.prod(mesh.shape[name] for name in axes)
        return lax.ppermute(values, axis, [(j, j ^ step) for j in range(size)])

    def near_of(values):
        return [values] + [hop(values, "sub", i) for i in range(1, n_sub)]

    def call(kernel, out_shape, smem, arrays, scratch=(), space=VMEM):
        return pl.pallas_call(
            kernel,
            out_shape=out_shape,
            in_specs=[SMEM] * len(smem) + [space] * len(arrays),
            out_specs=jax.tree.map(lambda _: VMEM, out_shape),
            scratch_shapes=list(scratch),
            compiler_params=pltpu.CompilerParams(vmem_limit_bytes=VMEM_LIMIT),
        )(*smem, *arrays)

    def per_device(points, weights, tile_rows, tile_count, sketch_pick, block_targets, core_inv):
        return body(points, weights, tile_rows, tile_count, sketch_pick, block_targets, core_inv)

    def body(points, weights, tile_rows, tile_count, sketch_pick, block_targets, core_inv):
        cap = tile_rows.shape[2]
        width, outs = points.shape[1], weights.shape[1]
        owners = tile_count.shape[1]
        live = owners * cap // 2
        quarter = live // n_sub // 2
        picks = sketch_pick.shape[1]

        def f32(*shape):
            return jax.ShapeDtypeStruct(shape, jnp.float32)

        def bf16(*shape):
            return jax.ShapeDtypeStruct(shape, jnp.bfloat16)

        own_x, row_ids, points = call(
            own_kernel,
            (bf16(cap, width), jax.ShapeDtypeStruct((1, cap), jnp.int32), bf16(*points.shape)),
            (),
            tuple(
                pltpu.with_memory_space_constraint(value, pltpu.MemorySpace.HBM)
                for value in (tile_rows[0], points)
            ),
            (pltpu.SemaphoreType.DMA(()), pltpu.SemaphoreType.DMA(())),
            pl.BlockSpec(memory_space=pltpu.MemorySpace.HBM),
        )
        far = [own_x] + [hop(own_x, "pts", i) for i in range(1, n_pts)]
        slabs = near_of(points)
        shift, turned = call(
            prep_kernel, (f32(cap, outs), bf16(outs, points.shape[0])), (),
            (row_ids, weights, block_targets[0]),
        )
        slab_ws = near_of(turned)
        shifts = near_of(shift)
        slab_sqs = [call(norm_kernel, f32(points.shape[0], 1), (), (slab,)) for slab in slabs]
        blocks = []
        for block in far:
            blocks += near_of(block)
        part, send, live_x = call(
            lambda *refs: slab_kernel(owners, n_sub, quarter, *refs),
            (f32(quarter, outs), f32(quarter, outs), bf16(live, width)),
            (tile_count,),
            (*blocks, *slabs, *slab_sqs, *slab_ws, *shifts),
            (pltpu.VMEM((live + cap + 8, width), jnp.float32), pltpu.VMEM((live + cap + 8, outs), jnp.float32)),
        )

        part = part + hop(send, "pts", 1)
        step = 2
        while step < n_pts:
            part = part + hop(part, "pts", step)
            step *= 2

        rows, share, sketch = call(
            lambda *refs: pick_kernel(2 * quarter, *refs),
            (bf16(2 * quarter, width), bf16(picks // n_sub, width), bf16(picks, width)),
            (),
            (sketch_pick, live_x),
        )
        got_sketch, got_rows = [], []
        for i in range(1, n_col):
            got_sketch += near_of(hop(share, "col", i))
        for i in range(1, n_col):
            got_rows += near_of(hop(rows, "col", i))

        def gram_shapes(groups):
            return tuple(bf16(cap, quarter * len(group)) for group in groups for _ in range(2))

        away = [(col, pts) for col in range(1, n_col) for pts in range(2)]
        near_groups = [
            [(0, 0, sub) for sub in range(n_sub)],
            [(0, 1, 0)],
            [(0, 1, sub) for sub in range(1, n_sub)],
        ]
        far_groups = [
            [(col, pts, 0) for col, pts in away],
            [(col, pts, sub) for col, pts in away for sub in range(1, n_sub)],
        ]
        near_grams = call(
            lambda *refs: near_gram_kernel(n_sub, n_col, quarter, near_groups, *refs),
            (bf16(n_col * picks, width), *(bf16(cap, n_col * picks),) * 2, *gram_shapes(near_groups)),
            (tile_count,),
            (own_x, live_x, sketch, core_inv, *got_sketch),
        )
        far_grams = call(
            lambda *refs: far_gram_kernel(n_sub, quarter, far_groups, *refs),
            gram_shapes(far_groups),
            (),
            (*near_grams[:3], *got_rows),
        )
        near_grams = near_grams[3:]
        grads = {}
        for sub, value in enumerate(near_of(part)):
            grads[0, 0, sub] = value
        for col, pts in [*reversed(away), (0, 1)]:
            other = hop(part, ("pts", "col"), pts * n_col + col)
            for sub, value in enumerate(near_of(other)):
                grads[col, pts, sub] = value

        def data(*groups):
            return [grads[key] for group in groups for key in group]

        early = [
            call(lambda *refs: part_kernel(1, *refs), f32(cap, outs), (),
                 (*near_grams[:2], *data(near_groups[0]))),
            call(lambda *refs: part_kernel(2, *refs), f32(cap, outs), (),
                 (*near_grams[2:4], *far_grams[:2], *data(near_groups[1], far_groups[0]))),
        ]
        block_grad, direction = call(
            lambda *refs: last_kernel(n_sub, len(early), 2, *refs),
            (f32(cap, outs), f32(cap, outs)),
            (tile_count,),
            (
                *early, *near_grams[4:], *far_grams[2:],
                *[grads[0, pts, sub] for pts in range(2) for sub in range(n_sub)],
                *data(near_groups[2], far_groups[1]),
            ),
            (pltpu.VMEM((live + cap + 8, outs), jnp.float32),),
        )
        return (block_grad[None], direction[None])

    return per_device


def solution(mesh):
    in_specs = (
        P(("grp", "pts", "sub"), None),
        P(("grp", "pts", "sub"), None),
        P(("grp", "col"), ("pts", "sub"), None),
        P(("grp", "col"), None),
        P(("grp", "col"), None),
        P(("grp", "col"), ("pts", "sub"), None),
        P("grp", None),
    )
    out_specs = (P(("grp", "col"), ("pts", "sub"), None), P(("grp", "col"), ("pts", "sub"), None))
    return jax.shard_map(
        make_device(mesh), mesh=mesh, in_specs=in_specs, out_specs=out_specs, check_vma=False
    )
```

```python
import math

import jax
import jax.numpy as jnp
from jax import lax
from jax.experimental import pallas as pl
from jax.experimental.pallas import tpu as pltpu
from jax.sharding import PartitionSpec as P

RIDGE_COEF = 50.0
LOG2E = 1.4426950408889634
VMEM_LIMIT = 24 << 20
SLAB_STEP = 512
ROWS_ROWS = (((1,), (1,)), ((), ()))
VMEM = pl.BlockSpec(memory_space=pltpu.VMEM)
SMEM = pl.BlockSpec(memory_space=pltpu.SMEM)


def split(values):
    high = values.astype(jnp.bfloat16)
    return high, (values - high.astype(jnp.float32)).astype(jnp.bfloat16)


def dot(left, right, dims=(((1,), (0,)), ((), ()))):
    return lax.dot_general(left, right, dims, preferred_element_type=jnp.float32)


def dot_parts(left, right, dims=(((1,), (0,)), ((), ()))):
    return dot(left[0], right[0], dims) + (dot(left[0], right[1], dims) + dot(left[1], right[0], dims))


def row_sq(points, scale):
    wide = points.astype(jnp.float32)
    high, low = split(wide * wide)
    ones = jnp.ones((8, points.shape[1]), jnp.bfloat16)
    return (dot(ones, high, ROWS_ROWS) + dot(ones, low, ROWS_ROWS))[:1] * scale


def col_sq(points, scale):
    wide = points.astype(jnp.float32)
    return jnp.sum(wide * wide, axis=1, keepdims=True) * scale


def as_column(row):
    lanes = 128
    square = [
        jnp.transpose(jnp.broadcast_to(row[:, at : at + lanes], (lanes, lanes)))[:, :1]
        for at in range(0, row.shape[1], lanes)
    ]
    return jnp.concatenate(square, axis=0)


def owner_span(counts, owner):
    off = jnp.int32(0)
    count = jnp.int32(0)
    for at in range(counts.shape[1]):
        here = counts[0, at]
        off = off + jnp.where(at < owner, here, 0)
        count = count + jnp.where(at == owner, here, 0)
    return off, count


def one_hot(row_ids, at, step):
    slot = lax.broadcasted_iota(jnp.int32, (row_ids.shape[0], step), 1) + at
    return (row_ids == slot).astype(jnp.float32).astype(jnp.bfloat16)


def own_kernel(
    n_sub, quarter, rows_hbm, points_hbm, counts_hbm,
    own_ref, rows_ref, points_ref, to_ref, counts, rows_sem, points_sem, counts_sem,
):
    total, width = points_ref.shape
    cap = own_ref.shape[0]
    step = math.gcd(total, 256)
    rows_copy = pltpu.make_async_copy(rows_hbm, rows_ref, rows_sem)
    points_copy = pltpu.make_async_copy(points_hbm, points_ref, points_sem)
    counts_copy = pltpu.make_async_copy(counts_hbm, counts, counts_sem)
    rows_copy.start()
    counts_copy.start()
    points_copy.start()
    rows_copy.wait()
    row_ids = as_column(rows_ref[...])
    hots = [one_hot(row_ids, at, step) for at in range(0, total, step)]
    counts_copy.wait()
    pts_at, sub_at = lax.axis_index("pts"), lax.axis_index("sub")
    turn = (sub_at * 2 + pts_at % 2) * quarter
    slot = lax.broadcasted_iota(jnp.int32, (1, cap), 1)
    for rel in range(to_ref.shape[0]):
        off, count = owner_span(counts, (pts_at * n_sub + sub_at) ^ rel)
        to_ref[rel : rel + 1, :] = jnp.where(slot < count, (slot + off) ^ turn, -1)
    points_copy.wait()
    own = jnp.zeros((cap, width), jnp.float32)
    for at, hot in enumerate(hots):
        own = own + dot(hot, points_ref[at * step : (at + 1) * step, :])
    own_ref[...] = own.astype(own_ref.dtype)


def hots_of(to_ref, rels, base, size):
    place = lax.broadcasted_iota(jnp.int32, (size, to_ref.shape[1]), 0) + base
    hots = [(place == to_ref[rel : rel + 1, :]).astype(jnp.float32).astype(jnp.bfloat16) for rel in rels]
    return jnp.concatenate(hots, axis=1)


def prep_kernel(rows_ref, weights_ref, targets_ref, to_ref, shift_ref, turned_ref, place_ref, hots_ref):
    place_ref[...] = one_hot(as_column(to_ref[:1, :]), 0, place_ref.shape[1])
    hots_ref[...] = hots_of(to_ref, range(to_ref.shape[0]), 0, hots_ref.shape[0])
    total = weights_ref.shape[0]
    step = math.gcd(total, 256)
    row_ids = as_column(rows_ref[...])
    alpha = jnp.zeros(shift_ref.shape, jnp.float32)
    for at in range(0, total, step):
        part = weights_ref[at : at + step, :]
        alpha = alpha + dot(one_hot(row_ids, at, step), part)
        turned_ref[:, at : at + step] = jnp.transpose(part.astype(jnp.float32)).astype(jnp.bfloat16)
    shift_ref[...] = RIDGE_COEF * alpha - targets_ref[...].astype(jnp.float32)


def norm_kernel(points_ref, sq_ref):
    sq_ref[...] = jnp.broadcast_to(col_sq(points_ref[...], LOG2E / points_ref.shape[1]), sq_ref.shape)


def three_parts(values):
    high, low = split(values)
    rest = values - high.astype(jnp.float32) - low.astype(jnp.float32)
    return high, low, rest.astype(jnp.bfloat16)


def shift_kernel(to_ref, *refs):
    parts = [three_parts(ref[...]) for ref in refs[:-1]]
    hots = hots_of(to_ref, range(len(parts)), 0, refs[-1].shape[0])
    refs[-1][...] = sum(dot(hots, jnp.concatenate(part, axis=0)) for part in zip(*parts))


def slab_kernel(n_blocks, n_sub, quarter, *refs):
    blocks, refs = refs[:n_blocks], refs[n_blocks:]
    slabs, slab_sqs, slab_ws = refs[:n_sub], refs[n_sub : 2 * n_sub], refs[2 * n_sub : 3 * n_sub]
    hots_ref, sums_ref, keep_ref, send_ref, mine_ref = refs[3 * n_sub :]
    scale = LOG2E / mine_ref.shape[1]
    points = jnp.concatenate([block[...] for block in blocks], axis=0)
    mine_x = dot(hots_ref[...], points).astype(jnp.bfloat16)
    mine_ref[...] = mine_x
    mine_sq = row_sq(mine_x, scale)
    total = jnp.zeros((keep_ref.shape[1], 2 * quarter), jnp.float32)
    step = math.gcd(slabs[0].shape[0], SLAB_STEP)
    for which in range(n_sub):
        for at in range(0, slabs[which].shape[0], step):
            inner = dot(slabs[which][at : at + step, :], mine_x, ROWS_ROWS)
            slab_sq = slab_sqs[which][at : at + step, :]
            slab_sq = jnp.concatenate([slab_sq] * (2 * quarter // slab_sq.shape[1]), axis=1)
            kern = jnp.exp2(inner * (2.0 * scale) - mine_sq - slab_sq)
            high, low = split(kern)
            turned = slab_ws[which][:, at : at + step]
            total = total + dot(turned, high) + dot(turned, low)
    total = jnp.transpose(total) + sums_ref[...]
    keep_ref[...] = total[:quarter]
    send_ref[...] = total[quarter:]


def pick_kernel(n_blocks, quarter, *refs):
    blocks, (to_ref, pick_ref, mine_ref, live_ref, sketch_ref) = refs[:n_blocks], refs[n_blocks:]
    live, half = live_ref.shape[0], mine_ref.shape[0]
    points = jnp.concatenate([block[...] for block in blocks], axis=0)
    live_ref[:half, :] = mine_ref[...]
    for base in range(half, live, half):
        hots = hots_of(to_ref, range(n_blocks), base, half)
        live_ref[base : base + half, :] = dot(hots, points).astype(jnp.bfloat16)
    turn = (lax.axis_index("sub") * 2 + lax.axis_index("pts") % 2) * quarter
    hot = one_hot(as_column(pick_ref[...] ^ turn), 0, live)
    sketch_ref[...] = dot(hot, live_ref[...]).astype(sketch_ref.dtype)


def sketch_rows(rows, points):
    scale = LOG2E / rows.shape[1]
    inner = dot(rows, points, ROWS_ROWS)
    return jnp.exp2(inner * (2.0 * scale) - col_sq(rows, scale) - row_sq(points, scale))


def write_groups(total, quarter, order, groups, outs):
    high, low = split(total)
    for at, group in enumerate(groups):
        for where, key in enumerate(group):
            base = order.index(key) * quarter
            outs[2 * at][:, where * quarter : (where + 1) * quarter] = high[:, base : base + quarter]
            outs[2 * at + 1][:, where * quarter : (where + 1) * quarter] = low[:, base : base + quarter]


def near_gram_kernel(n_sub, n_col, quarter, groups, *refs):
    own_ref, live_ref, to_ref, core_ref = refs[:4]
    sketches, refs = refs[4 : 4 + n_col], refs[4 + n_col :]
    mixed_high, mixed_low, outs = refs[0], refs[1], refs[2:]
    picks = sketches[0].shape[0]
    points = jnp.concatenate([ref[...] for ref in sketches], axis=0)
    used = as_column(to_ref[:1, :]) >= 0
    own = split(jnp.where(used, sketch_rows(own_ref[...], points), 0.0))
    col_at = lax.axis_index("col")
    tiles = [pl.ds(pl.multiple_of((col_at ^ col) * picks, picks), picks) for col in range(n_col)]
    core = [jnp.concatenate([core_ref[row, col] for col in tiles], axis=1) for row in tiles]
    mixed = split(dot_parts(own, split(jnp.concatenate(core, axis=0))))
    mixed_high[...], mixed_low[...] = mixed
    total = dot_parts(mixed, split(sketch_rows(live_ref[...], points)), ROWS_ROWS)
    order = [(0, pts, sub) for sub in range(n_sub) for pts in range(2)]
    write_groups(total, quarter, order, groups, outs)


def far_gram_kernel(n_sub, n_col, quarter, groups, *refs):
    mixed = refs[0][...], refs[1][...]
    sketches, refs = refs[2 : 2 + n_col], refs[2 + n_col :]
    got, outs = refs[: -2 * len(groups)], refs[-2 * len(groups) :]
    points = jnp.concatenate([ref[...] for ref in sketches], axis=0)
    rows = jnp.concatenate([ref[...] for ref in got], axis=0)
    total = dot_parts(mixed, split(sketch_rows(rows, points)), ROWS_ROWS)
    order = [(col, pts, sub) for col in range(1, n_col) for sub in range(n_sub) for pts in range(2)]
    write_groups(total, quarter, order, groups, outs)


def apply_grams(grams, parts):
    total, at = None, 0
    for high, low in grams:
        many = high.shape[1] // parts[0].shape[0]
        right = split(jnp.concatenate([ref[...] for ref in parts[at : at + many]], axis=0))
        term = dot_parts((high[...], low[...]), right)
        total = term if total is None else total + term
        at += many
    return total


def part_kernel(n_grams, *refs):
    grams = [refs[2 * at : 2 * at + 2] for at in range(n_grams)]
    refs[-1][...] = apply_grams(grams, refs[2 * n_grams : -1])


def tile_kernel(place_ref, *refs):
    rows = jnp.concatenate([ref[...] for ref in refs[:-1]], axis=0)
    refs[-1][...] = sum(dot(place_ref[...], part) for part in three_parts(rows))


def last_kernel(n_early, n_grams, *refs):
    early, refs = refs[: n_early + 1], refs[n_early + 1 :]
    grams, refs = [refs[2 * at : 2 * at + 2] for at in range(n_grams)], refs[2 * n_grams :]
    later, grad_ref, out_ref = refs[:-2], refs[-2], refs[-1]
    grad = early[0][...]
    grad_ref[...] = grad
    for ref in early[1:]:
        grad = grad - ref[...]
    out_ref[...] = grad - apply_grams(grams, later)


def make_device(mesh):
    n_pts, n_col, n_sub = mesh.shape["pts"], mesh.shape["col"], mesh.shape["sub"]

    def hop(values, axis, step):
        axes = axis if isinstance(axis, tuple) else (axis,)
        size = math.prod(mesh.shape[name] for name in axes)
        return lax.ppermute(values, axis, [(j, j ^ step) for j in range(size)])

    def near_of(values):
        return [values] + [hop(values, "sub", i) for i in range(1, n_sub)]

    def call(kernel, out_shape, smem, arrays, scratch=(), space=VMEM):
        return pl.pallas_call(
            kernel,
            out_shape=out_shape,
            in_specs=[SMEM] * len(smem) + [space] * len(arrays),
            out_specs=jax.tree.map(lambda _: VMEM, out_shape),
            scratch_shapes=list(scratch),
            compiler_params=pltpu.CompilerParams(vmem_limit_bytes=VMEM_LIMIT),
        )(*smem, *arrays)

    def per_device(points, weights, tile_rows, tile_count, sketch_pick, block_targets, core_inv):
        return body(points, weights, tile_rows, tile_count, sketch_pick, block_targets, core_inv)

    def body(points, weights, tile_rows, tile_count, sketch_pick, block_targets, core_inv):
        cap = tile_rows.shape[2]
        width, outs = points.shape[1], weights.shape[1]
        owners = tile_count.shape[1]
        live = owners * cap // 2
        quarter = live // n_sub // 2
        picks = sketch_pick.shape[1]

        def f32(*shape):
            return jax.ShapeDtypeStruct(shape, jnp.float32)

        def bf16(*shape):
            return jax.ShapeDtypeStruct(shape, jnp.bfloat16)

        own_x, row_ids, points, places = call(
            lambda *refs: own_kernel(n_sub, quarter, *refs),
            (
                bf16(cap, width),
                jax.ShapeDtypeStruct((1, cap), jnp.int32),
                bf16(*points.shape),
                jax.ShapeDtypeStruct((owners, cap), jnp.int32),
            ),
            (),
            tuple(
                pltpu.with_memory_space_constraint(value, pltpu.MemorySpace.HBM)
                for value in (tile_rows[0], points, tile_count)
            ),
            (pltpu.SMEM(tile_count.shape, jnp.int32), *(pltpu.SemaphoreType.DMA(()),) * 3),
            pl.BlockSpec(memory_space=pltpu.MemorySpace.HBM),
        )
        far = [own_x] + [hop(own_x, "pts", i) for i in range(1, n_pts)]
        slabs = near_of(points)
        shift, turned, own_place, hots = call(
            prep_kernel,
            (
                f32(cap, outs), bf16(outs, points.shape[0]),
                bf16(cap, live), bf16(2 * quarter, owners * cap),
            ),
            (),
            (row_ids, weights, block_targets[0], places),
        )
        slab_ws = near_of(turned)
        sums = call(shift_kernel, f32(2 * quarter, outs), (), (places, *near_of(shift)))
        slab_sqs = [call(norm_kernel, f32(points.shape[0], 128), (), (slab,)) for slab in slabs]
        blocks = []
        for block in far:
            blocks += near_of(block)
        part, send, mine_x = call(
            lambda *refs: slab_kernel(owners, n_sub, quarter, *refs),
            (f32(quarter, outs), f32(quarter, outs), bf16(2 * quarter, width)),
            (),
            (*blocks, *slabs, *slab_sqs, *slab_ws, hots, sums),
        )

        part = part + hop(send, "pts", 1)
        step = 2
        while step < n_pts:
            part = part + hop(part, "pts", step)
            step *= 2

        live_x, sketch = call(
            lambda *refs: pick_kernel(owners, quarter, *refs),
            (bf16(live, width), bf16(picks, width)),
            (),
            (*blocks, places, sketch_pick, mine_x),
        )
        got_sketch = [hop(sketch, "col", i) for i in range(1, n_col)]
        got_rows = []
        for i in range(1, n_col):
            got_rows += near_of(hop(mine_x, "col", i))

        def gram_shapes(groups):
            return tuple(bf16(cap, quarter * len(group)) for group in groups for _ in range(2))

        away = [(col, pts) for col in range(1, n_col) for pts in range(2)]
        near_groups = [
            [(0, 0, sub) for sub in range(n_sub)],
            [(0, 1, 0)],
            [(0, 1, sub) for sub in range(1, n_sub)],
        ]
        far_groups = [
            [(col, pts, 0) for col, pts in away],
            [(col, pts, sub) for col, pts in away for sub in range(1, n_sub)],
        ]
        near_grams = call(
            lambda *refs: near_gram_kernel(n_sub, n_col, quarter, near_groups, *refs),
            (*(bf16(cap, n_col * picks),) * 2, *gram_shapes(near_groups)),
            (),
            (own_x, live_x, places, core_inv, sketch, *got_sketch),
        )
        mixed, near_grams = near_grams[:2], near_grams[2:]
        far_grams = call(
            lambda *refs: far_gram_kernel(n_sub, n_col, quarter, far_groups, *refs),
            gram_shapes(far_groups),
            (),
            (*mixed, sketch, *got_sketch, *got_rows),
        )
        grads = {}
        for sub, value in enumerate(near_of(part)):
            grads[0, 0, sub] = value
        for col, pts in [*reversed(away), (0, 1)]:
            other = hop(part, ("pts", "col"), pts * n_col + col)
            for sub, value in enumerate(near_of(other)):
                grads[col, pts, sub] = value

        def data(*groups):
            return [grads[key] for group in groups for key in group]

        early = [
            call(lambda *refs: part_kernel(1, *refs), f32(cap, outs), (),
                 (*near_grams[:2], *data(near_groups[0]))),
            call(lambda *refs: part_kernel(2, *refs), f32(cap, outs), (),
                 (*near_grams[2:4], *far_grams[:2], *data(near_groups[1], far_groups[0]))),
        ]
        grad = call(
            tile_kernel, f32(cap, outs), (),
            (own_place, *[grads[0, pts, sub] for sub in range(n_sub) for pts in range(2)]),
        )
        block_grad, direction = call(
            lambda *refs: last_kernel(len(early), 2, *refs),
            (f32(cap, outs), f32(cap, outs)),
            (),
            (grad, *early, *near_grams[4:], *far_grams[2:], *data(near_groups[2], far_groups[1])),
        )
        return (block_grad[None], direction[None])

    return per_device


def solution(mesh):
    in_specs = (
        P(("grp", "pts", "sub"), None),
        P(("grp", "pts", "sub"), None),
        P(("grp", "col"), ("pts", "sub"), None),
        P(("grp", "col"), None),
        P(("grp", "col"), None),
        P(("grp", "col"), ("pts", "sub"), None),
        P("grp", None),
    )
    out_specs = (P(("grp", "col"), ("pts", "sub"), None), P(("grp", "col"), ("pts", "sub"), None))
    return jax.shard_map(
        make_device(mesh), mesh=mesh, in_specs=in_specs, out_specs=out_specs, check_vma=False
    )
```

```python
import math

import jax
import jax.numpy as jnp
from jax import lax
from jax.experimental import pallas as pl
from jax.experimental.pallas import tpu as pltpu
from jax.sharding import PartitionSpec as P

RIDGE_COEF = 50.0
LOG2E = 1.4426950408889634
VMEM_LIMIT = 24 << 20
SLAB_STEP = 512
OWN_CHUNKS = 1
ROWS_ROWS = (((1,), (1,)), ((), ()))
VMEM = pl.BlockSpec(memory_space=pltpu.VMEM)
SMEM = pl.BlockSpec(memory_space=pltpu.SMEM)


def split(values):
    high = values.astype(jnp.bfloat16)
    return high, (values - high.astype(jnp.float32)).astype(jnp.bfloat16)


def dot(left, right, dims=(((1,), (0,)), ((), ()))):
    return lax.dot_general(left, right, dims, preferred_element_type=jnp.float32)


def dot_parts(left, right, dims=(((1,), (0,)), ((), ()))):
    return dot(left[0], right[0], dims) + (dot(left[0], right[1], dims) + dot(left[1], right[0], dims))


def row_sq(points, scale):
    wide = points.astype(jnp.float32)
    high, low = split(wide * wide)
    ones = jnp.ones((8, points.shape[1]), jnp.bfloat16)
    return (dot(ones, high, ROWS_ROWS) + dot(ones, low, ROWS_ROWS))[:1] * scale


def col_sq(points, scale):
    wide = points.astype(jnp.float32)
    return jnp.sum(wide * wide, axis=1, keepdims=True) * scale


def as_column(row):
    lanes = 128
    square = [
        jnp.transpose(jnp.broadcast_to(row[:, at : at + lanes], (lanes, lanes)))[:, :1]
        for at in range(0, row.shape[1], lanes)
    ]
    return jnp.concatenate(square, axis=0)


def owner_span(counts, owner):
    off = jnp.int32(0)
    count = jnp.int32(0)
    for at in range(counts.shape[1]):
        here = counts[0, at]
        off = off + jnp.where(at < owner, here, 0)
        count = count + jnp.where(at == owner, here, 0)
    return off, count


def one_hot(row_ids, at, step):
    slot = lax.broadcasted_iota(jnp.int32, (row_ids.shape[0], step), 1) + at
    return (row_ids == slot).astype(jnp.float32).astype(jnp.bfloat16)


def own_kernel(
    n_sub, quarter, rows_hbm, points_hbm, counts_hbm, pick_hbm,
    own_ref, rows_ref, points_ref, to_ref, pick_ref, counts, rows_sem, counts_sem, pick_sem, points_sems,
):
    total, width = points_ref.shape
    cap = own_ref.shape[0]
    chunk = total // OWN_CHUNKS
    step = math.gcd(chunk, 256)
    rows_copy = pltpu.make_async_copy(rows_hbm, rows_ref, rows_sem)
    counts_copy = pltpu.make_async_copy(counts_hbm, counts, counts_sem)
    pick_copy = pltpu.make_async_copy(pick_hbm, pick_ref, pick_sem)
    points_copies = [
        pltpu.make_async_copy(
            points_hbm.at[pl.ds(at * chunk, chunk), :],
            points_ref.at[pl.ds(at * chunk, chunk), :],
            points_sems.at[at],
        )
        for at in range(OWN_CHUNKS)
    ]
    rows_copy.start()
    counts_copy.start()
    for copy in points_copies:
        copy.start()
    pick_copy.start()
    rows_copy.wait()
    row_ids = as_column(rows_ref[...])
    hots = [one_hot(row_ids, at, step) for at in range(0, total, step)]
    counts_copy.wait()
    pts_at, sub_at = lax.axis_index("pts"), lax.axis_index("sub")
    turn = (sub_at * 2 + pts_at % 2) * quarter
    slot = lax.broadcasted_iota(jnp.int32, (1, cap), 1)
    for rel in range(to_ref.shape[0]):
        off, count = owner_span(counts, (pts_at * n_sub + sub_at) ^ rel)
        to_ref[rel : rel + 1, :] = jnp.where(slot < count, (slot + off) ^ turn, -1)
    own = jnp.zeros((cap, width), jnp.float32)
    for at, hot in enumerate(hots):
        if at * step % chunk == 0:
            points_copies[at * step // chunk].wait()
        own = own + dot(hot, points_ref[at * step : (at + 1) * step, :])
    own_ref[...] = own.astype(own_ref.dtype)
    pick_copy.wait()


def hots_of(to_ref, rels, base, size):
    place = lax.broadcasted_iota(jnp.int32, (size, to_ref.shape[1]), 0) + base
    hots = [(place == to_ref[rel : rel + 1, :]).astype(jnp.float32).astype(jnp.bfloat16) for rel in rels]
    return jnp.concatenate(hots, axis=1)


def prep_kernel(
    quarter, rows_ref, weights_ref, targets_ref, to_ref, pick_ref,
    shift_ref, turned_ref, place_ref, hots_ref, picks_ref,
):
    place_ref[...] = one_hot(as_column(to_ref[:1, :]), 0, place_ref.shape[1])
    hots_ref[...] = hots_of(to_ref, range(to_ref.shape[0]), 0, hots_ref.shape[0])
    turn = (lax.axis_index("sub") * 2 + lax.axis_index("pts") % 2) * quarter
    picks_ref[...] = one_hot(as_column(pick_ref[...] ^ turn), 0, picks_ref.shape[1])
    total = weights_ref.shape[0]
    step = math.gcd(total, 256)
    row_ids = as_column(rows_ref[...])
    alpha = jnp.zeros(shift_ref.shape, jnp.float32)
    for at in range(0, total, step):
        part = weights_ref[at : at + step, :]
        alpha = alpha + dot(one_hot(row_ids, at, step), part)
        turned_ref[:, at : at + step] = jnp.transpose(part.astype(jnp.float32)).astype(jnp.bfloat16)
    shift_ref[...] = RIDGE_COEF * alpha - targets_ref[...].astype(jnp.float32)


def norm_kernel(points_ref, sq_ref):
    sq_ref[...] = jnp.broadcast_to(col_sq(points_ref[...], LOG2E / points_ref.shape[1]), sq_ref.shape)


def three_parts(values):
    high, low = split(values)
    rest = values - high.astype(jnp.float32) - low.astype(jnp.float32)
    return high, low, rest.astype(jnp.bfloat16)


def shift_kernel(to_ref, *refs):
    parts = [three_parts(ref[...]) for ref in refs[:-1]]
    hots = hots_of(to_ref, range(len(parts)), 0, refs[-1].shape[0])
    refs[-1][...] = sum(dot(hots, jnp.concatenate(part, axis=0)) for part in zip(*parts))


def most_kernel(late, hots_ref, *refs):
    blocks, out_ref = refs[:-1], refs[-1]
    cap = blocks[0].shape[0]
    hots = jnp.concatenate([hots_ref[:, : late * cap], hots_ref[:, (late + 1) * cap :]], axis=1)
    out_ref[...] = dot(hots, jnp.concatenate([block[...] for block in blocks], axis=0))


def slab_kernel(late, n_sub, quarter, block_ref, most_ref, *refs):
    slabs, slab_sqs, slab_ws = refs[:n_sub], refs[n_sub : 2 * n_sub], refs[2 * n_sub : 3 * n_sub]
    hots_ref, sums_ref, keep_ref, send_ref, mine_ref = refs[3 * n_sub :]
    scale = LOG2E / mine_ref.shape[1]
    cap = block_ref.shape[0]
    hots = hots_ref[:, late * cap : (late + 1) * cap]
    mine_x = (most_ref[...] + dot(hots, block_ref[...])).astype(jnp.bfloat16)
    mine_ref[...] = mine_x
    mine_sq = row_sq(mine_x, scale)
    total = jnp.zeros((keep_ref.shape[1], 2 * quarter), jnp.float32)
    step = math.gcd(slabs[0].shape[0], SLAB_STEP)
    for which in range(n_sub):
        for at in range(0, slabs[which].shape[0], step):
            inner = dot(slabs[which][at : at + step, :], mine_x, ROWS_ROWS)
            slab_sq = slab_sqs[which][at : at + step, :]
            slab_sq = jnp.concatenate([slab_sq] * (2 * quarter // slab_sq.shape[1]), axis=1)
            kern = jnp.exp2(inner * (2.0 * scale) - mine_sq - slab_sq)
            high, low = split(kern)
            turned = slab_ws[which][:, at : at + step]
            total = total + dot(turned, high) + dot(turned, low)
    total = jnp.transpose(total) + sums_ref[...]
    keep_ref[...] = total[:quarter]
    send_ref[...] = total[quarter:]


def pick_kernel(n_blocks, *refs):
    blocks, (to_ref, picks_ref, mine_ref, live_ref, sketch_ref) = refs[:n_blocks], refs[n_blocks:]
    live, half = live_ref.shape[0], mine_ref.shape[0]
    points = jnp.concatenate([block[...] for block in blocks], axis=0)
    live_ref[:half, :] = mine_ref[...]
    for base in range(half, live, half):
        hots = hots_of(to_ref, range(n_blocks), base, half)
        live_ref[base : base + half, :] = dot(hots, points).astype(jnp.bfloat16)
    sketch_ref[...] = dot(picks_ref[...], live_ref[...]).astype(sketch_ref.dtype)


def sketch_rows(rows, points):
    scale = LOG2E / rows.shape[1]
    inner = dot(rows, points, ROWS_ROWS)
    return jnp.exp2(inner * (2.0 * scale) - col_sq(rows, scale) - row_sq(points, scale))


def write_groups(total, quarter, order, groups, outs):
    high, low = split(total)
    for at, group in enumerate(groups):
        for where, key in enumerate(group):
            base = order.index(key) * quarter
            outs[2 * at][:, where * quarter : (where + 1) * quarter] = high[:, base : base + quarter]
            outs[2 * at + 1][:, where * quarter : (where + 1) * quarter] = low[:, base : base + quarter]


def near_gram_kernel(n_sub, n_col, quarter, groups, *refs):
    own_ref, live_ref, to_ref, core_ref = refs[:4]
    sketches, refs = refs[4 : 4 + n_col], refs[4 + n_col :]
    mixed_high, mixed_low, outs = refs[0], refs[1], refs[2:]
    picks = sketches[0].shape[0]
    points = jnp.concatenate([ref[...] for ref in sketches], axis=0)
    used = as_column(to_ref[:1, :]) >= 0
    own = split(jnp.where(used, sketch_rows(own_ref[...], points), 0.0))
    col_at = lax.axis_index("col")
    tiles = [pl.ds(pl.multiple_of((col_at ^ col) * picks, picks), picks) for col in range(n_col)]
    core = [jnp.concatenate([core_ref[row, col] for col in tiles], axis=1) for row in tiles]
    mixed = split(dot_parts(own, split(jnp.concatenate(core, axis=0))))
    mixed_high[...], mixed_low[...] = mixed
    total = dot_parts(mixed, split(sketch_rows(live_ref[...], points)), ROWS_ROWS)
    order = [(0, pts, sub) for sub in range(n_sub) for pts in range(2)]
    write_groups(total, quarter, order, groups, outs)


def far_gram_kernel(n_sub, n_col, quarter, groups, *refs):
    mixed = refs[0][...], refs[1][...]
    sketches, refs = refs[2 : 2 + n_col], refs[2 + n_col :]
    got, outs = refs[: -2 * len(groups)], refs[-2 * len(groups) :]
    points = jnp.concatenate([ref[...] for ref in sketches], axis=0)
    rows = jnp.concatenate([ref[...] for ref in got], axis=0)
    total = dot_parts(mixed, split(sketch_rows(rows, points)), ROWS_ROWS)
    order = [(col, pts, sub) for col in range(1, n_col) for sub in range(n_sub) for pts in range(2)]
    write_groups(total, quarter, order, groups, outs)


def apply_grams(grams, parts):
    total, at = None, 0
    for high, low in grams:
        many = high.shape[1] // parts[0].shape[0]
        right = split(jnp.concatenate([ref[...] for ref in parts[at : at + many]], axis=0))
        term = dot_parts((high[...], low[...]), right)
        total = term if total is None else total + term
        at += many
    return total


def part_kernel(n_grams, *refs):
    grams = [refs[2 * at : 2 * at + 2] for at in range(n_grams)]
    refs[-1][...] = apply_grams(grams, refs[2 * n_grams : -1])


def tile_kernel(place_ref, *refs):
    rows = jnp.concatenate([ref[...] for ref in refs[:-1]], axis=0)
    refs[-1][...] = sum(dot(place_ref[...], part) for part in three_parts(rows))


def last_kernel(n_early, n_grams, *refs):
    early, refs = refs[: n_early + 1], refs[n_early + 1 :]
    grams, refs = [refs[2 * at : 2 * at + 2] for at in range(n_grams)], refs[2 * n_grams :]
    later, grad_ref, out_ref = refs[:-2], refs[-2], refs[-1]
    grad = early[0][...]
    grad_ref[...] = grad
    for ref in early[1:]:
        grad = grad - ref[...]
    out_ref[...] = grad - apply_grams(grams, later)


def make_device(mesh):
    n_pts, n_col, n_sub = mesh.shape["pts"], mesh.shape["col"], mesh.shape["sub"]

    def hop(values, axis, step):
        axes = axis if isinstance(axis, tuple) else (axis,)
        size = math.prod(mesh.shape[name] for name in axes)
        return lax.ppermute(values, axis, [(j, j ^ step) for j in range(size)])

    def near_of(values):
        return [values] + [hop(values, "sub", i) for i in range(1, n_sub)]

    def call(kernel, out_shape, smem, arrays, scratch=(), space=VMEM):
        return pl.pallas_call(
            kernel,
            out_shape=out_shape,
            in_specs=[SMEM] * len(smem) + [space] * len(arrays),
            out_specs=jax.tree.map(lambda _: VMEM, out_shape),
            scratch_shapes=list(scratch),
            compiler_params=pltpu.CompilerParams(vmem_limit_bytes=VMEM_LIMIT),
        )(*smem, *arrays)

    def per_device(points, weights, tile_rows, tile_count, sketch_pick, block_targets, core_inv):
        return body(points, weights, tile_rows, tile_count, sketch_pick, block_targets, core_inv)

    def body(points, weights, tile_rows, tile_count, sketch_pick, block_targets, core_inv):
        cap = tile_rows.shape[2]
        width, outs = points.shape[1], weights.shape[1]
        owners = tile_count.shape[1]
        live = owners * cap // 2
        quarter = live // n_sub // 2
        picks = sketch_pick.shape[1]

        def f32(*shape):
            return jax.ShapeDtypeStruct(shape, jnp.float32)

        def bf16(*shape):
            return jax.ShapeDtypeStruct(shape, jnp.bfloat16)

        own_x, row_ids, points, places, pick_ids = call(
            lambda *refs: own_kernel(n_sub, quarter, *refs),
            (
                bf16(cap, width),
                jax.ShapeDtypeStruct((1, cap), jnp.int32),
                bf16(*points.shape),
                jax.ShapeDtypeStruct((owners, cap), jnp.int32),
                jax.ShapeDtypeStruct(sketch_pick.shape, jnp.int32),
            ),
            (),
            tuple(
                pltpu.with_memory_space_constraint(value, pltpu.MemorySpace.HBM)
                for value in (tile_rows[0], points, tile_count, sketch_pick)
            ),
            (
                pltpu.SMEM(tile_count.shape, jnp.int32),
                *(pltpu.SemaphoreType.DMA(()),) * 3,
                pltpu.SemaphoreType.DMA((OWN_CHUNKS,)),
            ),
            pl.BlockSpec(memory_space=pltpu.MemorySpace.HBM),
        )
        far = [own_x] + [hop(own_x, "pts", i) for i in range(1, n_pts)]
        slabs = near_of(points)
        shift, turned, own_place, hots, pick_hots = call(
            lambda *refs: prep_kernel(quarter, *refs),
            (
                f32(cap, outs), bf16(outs, points.shape[0]),
                bf16(cap, live), bf16(2 * quarter, owners * cap), bf16(picks, live),
            ),
            (),
            (row_ids, weights, block_targets[0], places, pick_ids),
        )
        slab_ws = near_of(turned)
        sums = call(shift_kernel, f32(2 * quarter, outs), (), (places, *near_of(shift)))
        slab_sqs = [call(norm_kernel, f32(points.shape[0], 128), (), (slab,)) for slab in slabs]
        blocks = []
        for block in far:
            blocks += near_of(block)
        late = min(3 * n_sub, owners) - 1
        most = call(
            lambda *refs: most_kernel(late, *refs),
            f32(2 * quarter, width),
            (),
            (hots, *blocks[:late], *blocks[late + 1 :]),
        )
        part, send, mine_x = call(
            lambda *refs: slab_kernel(late, n_sub, quarter, *refs),
            (f32(quarter, outs), f32(quarter, outs), bf16(2 * quarter, width)),
            (),
            (blocks[late], most, *slabs, *slab_sqs, *slab_ws, hots, sums),
        )

        part = part + hop(send, "pts", 1)
        step = 2
        while step < n_pts:
            part = part + hop(part, "pts", step)
            step *= 2

        live_x, sketch = call(
            lambda *refs: pick_kernel(owners, *refs),
            (bf16(live, width), bf16(picks, width)),
            (),
            (*blocks, places, pick_hots, mine_x),
        )
        got_sketch = [hop(sketch, "col", i) for i in range(1, n_col)]
        got_rows = []
        for i in range(1, n_col):
            got_rows += near_of(hop(mine_x, "col", i))

        def gram_shapes(groups):
            return tuple(bf16(cap, quarter * len(group)) for group in groups for _ in range(2))

        away = [(col, pts) for col in range(1, n_col) for pts in range(2)]
        near_groups = [
            [(0, 0, sub) for sub in range(n_sub)],
            [(0, 1, 0)],
            [(0, 1, sub) for sub in range(1, n_sub)],
        ]
        far_groups = [
            [(col, pts, 0) for col, pts in away],
            [(col, pts, sub) for col, pts in away for sub in range(1, n_sub)],
        ]
        near_grams = call(
            lambda *refs: near_gram_kernel(n_sub, n_col, quarter, near_groups, *refs),
            (*(bf16(cap, n_col * picks),) * 2, *gram_shapes(near_groups)),
            (),
            (own_x, live_x, places, core_inv, sketch, *got_sketch),
        )
        mixed, near_grams = near_grams[:2], near_grams[2:]
        far_grams = call(
            lambda *refs: far_gram_kernel(n_sub, n_col, quarter, far_groups, *refs),
            gram_shapes(far_groups),
            (),
            (*mixed, sketch, *got_sketch, *got_rows),
        )
        grads = {}
        for sub, value in enumerate(near_of(part)):
            grads[0, 0, sub] = value
        for col, pts in [*reversed(away), (0, 1)]:
            other = hop(part, ("pts", "col"), pts * n_col + col)
            for sub, value in enumerate(near_of(other)):
                grads[col, pts, sub] = value

        def data(*groups):
            return [grads[key] for group in groups for key in group]

        early = [
            call(lambda *refs: part_kernel(1, *refs), f32(cap, outs), (),
                 (*near_grams[:2], *data(near_groups[0]))),
            call(lambda *refs: part_kernel(2, *refs), f32(cap, outs), (),
                 (*near_grams[2:4], *far_grams[:2], *data(near_groups[1], far_groups[0]))),
        ]
        grad = call(
            tile_kernel, f32(cap, outs), (),
            (own_place, *[grads[0, pts, sub] for sub in range(n_sub) for pts in range(2)]),
        )
        block_grad, direction = call(
            lambda *refs: last_kernel(len(early), 2, *refs),
            (f32(cap, outs), f32(cap, outs)),
            (),
            (grad, *early, *near_grams[4:], *far_grams[2:], *data(near_groups[2], far_groups[1])),
        )
        return (block_grad[None], direction[None])

    return per_device


def solution(mesh):
    in_specs = (
        P(("grp", "pts", "sub"), None),
        P(("grp", "pts", "sub"), None),
        P(("grp", "col"), ("pts", "sub"), None),
        P(("grp", "col"), None),
        P(("grp", "col"), None),
        P(("grp", "col"), ("pts", "sub"), None),
        P("grp", None),
    )
    out_specs = (P(("grp", "col"), ("pts", "sub"), None), P(("grp", "col"), ("pts", "sub"), None))
    return jax.shard_map(
        make_device(mesh), mesh=mesh, in_specs=in_specs, out_specs=out_specs, check_vma=False
    )
```
